32 devices in a mesh: groups: 2 (over y), seq: 16 (over z, x, core).
Axes of the slice: x: 2, y: 2, z: 4, core: 2. Of those that a mesh axis runs over, the one named last changes fastest.
Arguments:
- span_frames: bfloat16 [512, 512], P(('groups', 'seq')), parts along dimension 0, may hold values from -3 to 3
- query_rows: bfloat16 [512, 512], P(('groups', 'seq')), parts along dimension 0, may hold values from -12 to 12
- key_rows: bfloat16 [16384, 512], P(('groups', 'seq')), parts along dimension 0, may hold values from -6 to 6
- context_frames: bfloat16 [16384, 512], P(('groups', 'seq')), parts along dimension 0, may hold values from -6 to 6
- key_mask: int32 [16384], P(('groups', 'seq')), parts along dimension 0, may hold values from 0 to 1, as said below
- value_weight: bfloat16 [512, 512], replicated, may hold values from -0.5 to 0.5
- out_weight: bfloat16 [512, 512], replicated, may hold values from -0.25 to 0.25
- expand_weight: bfloat16 [512, 1024], replicated, may hold values from -0.25 to 0.25
- depth_weight: float32 [31, 512], replicated, may hold values from -1 to 1
- norm_scale: float32 [512], replicated, may hold values from 0.5 to 2
- norm_shift: float32 [512], replicated, may hold values from -3 to 3
- project_weight: bfloat16 [512, 512], replicated, may hold values from -0.25 to 0.25
Outputs:
- layer_out: bfloat16 [512, 512], P(('groups', 'seq')), parts along dimension 0
The draws below stay inside these ranges and needn't reach their ends.
There are 2 independent parts, one for each index of `groups`. The reference program is written for one: setup_inputs(seed, part) draws one part's arguments, and reference() takes and returns one part's arrays. A program takes and returns all parts, laid end to end along the dimension named above; an argument that names none is the same for every part. Nothing has to cross between parts.
Inputs may be any that keep to these rules, and one draw needn't show every extreme that they name: `key_mask`: within each block of 512 frames held by one index of seq, the real frames come first and there is at least one.
All inputs are finite; a program needn't handle non-finite values.
Results may differ from the reference program's by a relative error of at most 0.013.
Values may be sent and summed in bfloat16 or wider, within the bound.
A program may use at most 384 MiB of HBM per device.

```python
import math
import jax
import jax.numpy as jnp
from jax import lax

D = 512
HEADS = 8
HEAD_DIM = 64
KERNEL = 31
HALF = 15
KV_DEV = 512
QUERIES = 256
KEYS = 8192


def drawn_pair(key):
    key_part = jax.random.fold_in(key, 101)
    query_part = jax.random.fold_in(key, 202)
    key_table = jnp.clip(1.7 * jax.random.normal(key_part, (KEYS, D), jnp.float32), -6.0, 6.0)
    query_table = jnp.clip(1.7 * jax.random.normal(query_part, (QUERIES, D), jnp.float32), -6.0, 6.0)
    return (key_table, query_table)


def draw_key_rows(key, part):
    return drawn_pair(key)[0].astype(jnp.bfloat16)


def draw_query_rows(key, part):
    return drawn_pair(key)[1].astype(jnp.bfloat16)


def draw_key_mask(key, part):
    lengths = jax.random.randint(jax.random.fold_in(key, 404), (KEYS // KV_DEV,), KV_DEV // 4, KV_DEV + 1, dtype=jnp.int32)
    frame = jnp.arange(KEYS, dtype=jnp.int32)
    return (frame % KV_DEV < lengths[frame // KV_DEV]).astype(jnp.int32)


def block_levels(key, extent, split, smallest, largest):
    def one(dim, blocks):
        steps = jax.random.uniform(jax.random.fold_in(jax.random.fold_in(key, 6), dim), (blocks,), jnp.float32, smallest / len(split), largest / len(split))
        return jnp.repeat(jnp.exp(steps), extent[dim] // blocks).reshape((-1,) + (1,) * (len(extent) - dim - 1))

    factor_of = one(*split[0])
    for cut in split[1:]:
        factor_of = factor_of * one(*cut)
    return factor_of


def normal_values(key, dims, scale, most, cuts=(), kind=jnp.bfloat16):
    drawn = scale * jax.random.normal(key, dims, jnp.float32)
    if cuts:
        drawn = drawn * block_levels(key, dims, cuts, -0.22, 0.18)
    return jnp.clip(drawn, -most, most).astype(kind)


def setup_inputs(seed: int = 0, part: int = 0) -> dict:
    splits = jax.random.split(jax.random.key(seed), 13)
    part_splits = jax.random.split(jax.random.fold_in(splits[12], part), 13)
    span_frames = normal_values(part_splits[0], (QUERIES, D), 0.5, 3.0, ((0, 16),))
    query_rows = draw_query_rows(jax.random.fold_in(jax.random.fold_in(splits[12], part), 71), part)
    key_rows = draw_key_rows(jax.random.fold_in(jax.random.fold_in(splits[12], part), 71), part)
    context_frames = normal_values(part_splits[3], (KEYS, D), 1.0, 6.0, ((0, 16),))
    key_mask = draw_key_mask(jax.random.fold_in(jax.random.fold_in(splits[12], part), 71), part)
    value_weight = normal_values(splits[5], (D, D), (D // 4) ** -0.5, 0.5)
    out_weight = normal_values(splits[6], (D, D), D ** -0.5, 0.25)
    expand_weight = normal_values(splits[7], (D, 2 * D), D ** -0.5, 0.25)
    depth_weight = normal_values(splits[8], (KERNEL, D), KERNEL ** -0.5, 1.0, (), jnp.float32)
    norm_scale = jnp.clip(jnp.exp(jax.random.uniform(splits[9], (D,), jnp.float32, math.log(0.5), math.log(2.0))), 0.5, 2.0)
    norm_shift = normal_values(splits[10], (D,), 0.5, 3.0, (), jnp.float32)
    project_weight = normal_values(splits[11], (D, D), D ** -0.5, 0.25)
    return {"span_frames": span_frames, "query_rows": query_rows, "key_rows": key_rows, "context_frames": context_frames, "key_mask": key_mask, "value_weight": value_weight, "out_weight": out_weight, "expand_weight": expand_weight, "depth_weight": depth_weight, "norm_scale": norm_scale, "norm_shift": norm_shift, "project_weight": project_weight}


def attend_all(query_rows, key_rows, values, key_mask):
    valid = key_mask > 0
    scale = 1.0 / math.sqrt(HEAD_DIM)
    block = min(128, QUERIES)

    def one_head(head):
        query_head = lax.dynamic_slice_in_dim(query_rows, head * HEAD_DIM, HEAD_DIM, 1)
        key_head = lax.dynamic_slice_in_dim(key_rows, head * HEAD_DIM, HEAD_DIM, 1)
        value_head = lax.dynamic_slice_in_dim(values, head * HEAD_DIM, HEAD_DIM, 1)

        def one_block(query_block):
            scores = jnp.dot(query_block, key_head.T, preferred_element_type=jnp.float32) * scale
            scores = jnp.where(valid[None, :], scores, -1e+30)
            top = lax.optimization_barrier(jnp.max(scores, axis=1))
            weights = jnp.exp(scores - top[:, None])
            weights = jnp.where(valid[None, :], weights, 0.0)
            total = lax.optimization_barrier(jnp.sum(weights, axis=1))
            summed = jnp.dot(weights.astype(jnp.bfloat16), value_head, preferred_element_type=jnp.float32)
            return summed / total[:, None]
        outputs = lax.map(one_block, query_head.reshape(QUERIES // block, block, HEAD_DIM))
        return outputs.reshape(QUERIES, HEAD_DIM)
    per_head = lax.map(one_head, jnp.arange(HEADS, dtype=jnp.int32))
    return jnp.transpose(per_head, (1, 0, 2)).reshape(QUERIES, D).astype(jnp.bfloat16)

def reference(span_frames, query_rows, key_rows, context_frames, key_mask, value_weight, out_weight, expand_weight, depth_weight, norm_scale, norm_shift, project_weight):
    values = jnp.dot(context_frames, value_weight, preferred_element_type=jnp.float32).astype(jnp.bfloat16)
    attended = attend_all(query_rows, key_rows, values, key_mask)
    mixed = (span_frames.astype(jnp.float32) + jnp.dot(attended, out_weight, preferred_element_type=jnp.float32)).astype(jnp.bfloat16)
    wide = mixed.astype(jnp.float32)
    centre = lax.optimization_barrier(jnp.mean(wide, axis=1, keepdims=True))
    spread = lax.optimization_barrier(jnp.mean((wide - centre) ** 2, axis=1, keepdims=True))
    normed = ((wide - centre) / jnp.sqrt(spread + 1e-05)).astype(jnp.bfloat16)
    expanded = jnp.dot(normed, expand_weight, preferred_element_type=jnp.float32)
    gated = (expanded[:, :D] * jax.nn.sigmoid(expanded[:, D:])).astype(jnp.bfloat16)
    padded = jnp.pad(gated.astype(jnp.float32), ((HALF, HALF), (0, 0)))
    conv = jnp.zeros((QUERIES, D), jnp.float32)
    for offset in range(KERNEL):
        conv = conv + padded[offset:offset + QUERIES] * depth_weight[offset][None, :]
    normal_conv = conv * norm_scale[None, :] + norm_shift[None, :]
    activated = (normal_conv * jax.nn.sigmoid(normal_conv)).astype(jnp.bfloat16)
    return (wide + jnp.dot(activated, project_weight, preferred_element_type=jnp.float32)).astype(jnp.bfloat16)
```

```python
import functools

import jax
import jax.numpy as jnp
from jax import lax
from jax.experimental import pallas as pl
from jax.experimental.pallas import tpu as pltpu
from jax.sharding import PartitionSpec as P

HEADS = 8
CORES = 2
MESH = pl.DeviceIdType.MESH
F32 = jnp.float32
BF16 = jnp.bfloat16


def dot(a, b):
    return jnp.dot(a, b, preferred_element_type=F32)


def layer_kernel(
    n,
    group,
    span_hbm,
    query_hbm,
    key_hbm,
    context_hbm,
    mask_hbm,
    value_w_hbm,
    out_w_hbm,
    expand_w_hbm,
    depth_hbm,
    scale_hbm,
    shift_hbm,
    project_w_hbm,
    out_ref,
    span,
    own_query,
    keys,
    context,
    mask,
    value_w,
    out_w,
    expand_w,
    depth,
    norm_scale,
    norm_shift,
    project_w,
    value_out,
    values,
    queries,
    partial_out,
    partials,
    spread,
    bias,
    gated,
    halo,
    padded,
    load_sem,
    query_send,
    query_recv,
    part_send,
    part_recv,
    pair_send,
    pair_recv,
    halo_send,
    halo_recv,
):
    me = lax.axis_index("seq")
    core = lax.rem(me, CORES)
    other = 1 - core
    pair = me - core + other
    rows, width = span.shape
    half = width // CORES
    frames = context.shape[0]
    heads = HEADS // CORES
    head_dim = width // HEADS
    block_rows = group * rows
    blocks = n // group
    lane_slot = 128 // heads

    barrier = pltpu.get_barrier_semaphore()

    def greet(step, carry):
        peer = lax.rem(me + step, n)
        pl.semaphore_signal(barrier, inc=1, device_id={"seq": peer}, device_id_type=MESH)
        return carry

    lax.fori_loop(1, n, greet, 0)

    def columns(index):
        return pl.ds(pl.multiple_of(index * half, half), half)

    loads = []

    def load(src, dst):
        copy = pltpu.make_async_copy(src, dst, load_sem.at[len(loads)])
        copy.start()
        loads.append(copy)
        return copy

    load_context = load(context_hbm, context)
    load_value_w = load(value_w_hbm, value_w)
    load_query = [load(query_hbm.at[:, i * half : (i + 1) * half], own_query.at[i]) for i in range(CORES)]
    load_mask = load(mask_hbm, mask.at[core])
    load_keys = load(key_hbm.at[:, columns(core)], keys.at[core])
    load_rest = [
        load(src, dst)
        for src, dst in (
            (span_hbm, span),
            (out_w_hbm, out_w),
            (expand_w_hbm, expand_w),
            (depth_hbm, depth),
            (scale_hbm, norm_scale),
            (shift_hbm, norm_shift),
            (project_w_hbm, project_w),
        )
    ]

    load_context.wait()
    load_value_w.wait()
    value_out[...] = dot(context[...], value_w[:, columns(other)]).astype(BF16)
    for copy in load_query:
        copy.wait()
    load_mask.wait()

    pl.semaphore_wait(barrier, n - 1)

    def remote(src, dst, send, recv, peer):
        return pltpu.make_async_remote_copy(
            src_ref=src,
            dst_ref=dst,
            send_sem=send,
            recv_sem=recv,
            device_id={"seq": peer},
            device_id_type=MESH,
        )

    def query_copy(peer, slot, sem_index):
        return remote(
            own_query.at[lax.rem(peer, CORES)],
            queries.at[slot],
            query_send.at[sem_index],
            query_recv.at[slot],
            peer,
        )

    key_copy = remote(
        key_hbm.at[:, columns(other)], keys.at[core], pair_send.at[0], pair_recv.at[0], pair
    )
    mask_copy = remote(mask.at[core], mask.at[core], pair_send.at[1], pair_recv.at[1], pair)
    value_copy = remote(value_out, values.at[core], pair_send.at[2], pair_recv.at[2], pair)
    key_copy.start()
    mask_copy.start()

    def send_query(step, carry):
        peer = lax.rem(me + step, n)
        query_copy(peer, me, peer).start()
        return carry

    lax.fori_loop(1, n, send_query, 0)
    value_copy.start()

    values[core] = dot(context[...], value_w[:, columns(core)]).astype(BF16)
    queries[me] = own_query[core]
    slot_row = lax.broadcasted_iota(jnp.int32, (128, 2 * half), 0)
    slot_col = lax.broadcasted_iota(jnp.int32, (128, 2 * half), 1)
    slot_head = lax.rem(slot_col, half) // head_dim * lane_slot
    shift_pick = jnp.logical_and(slot_col < half, slot_row == slot_head)
    total_pick = jnp.logical_and(
        slot_col >= half,
        jnp.logical_or(
            slot_row == slot_head + lane_slot // 2, slot_row == slot_head + lane_slot * 3 // 4
        ),
    )
    spread[...] = jnp.where(jnp.logical_or(shift_pick, total_pick), 1.0, 0.0).astype(BF16)

    load_keys.wait()
    remote(keys.at[other], keys.at[other], pair_send.at[0], pair_recv.at[0], pair).wait_recv()
    remote(mask.at[other], mask.at[other], pair_send.at[1], pair_recv.at[1], pair).wait_recv()
    for i in range(CORES):
        bias[:, i * frames : (i + 1) * frames] = jnp.where(mask[i] > 0, 0.0, -1e30)
    remote(values.at[other], values.at[other], pair_send.at[2], pair_recv.at[2], pair).wait_recv()

    head_lane = lax.broadcasted_iota(jnp.int32, (1, half), 1) // head_dim
    stat_lane = lax.broadcasted_iota(jnp.int32, (1, 128), 1)
    first_block = me // group
    heading = 1 - 2 * (2 * first_block // blocks)

    def attend(step, carry):
        block = lax.rem(first_block + heading * step + blocks, blocks)
        for i in range(group):
            source = block * group + i

            @pl.when(source != me)
            def _():
                query_copy(pair, source, source).wait_recv()

        query = queries[pl.ds(block * group, group)].reshape(block_rows, half)
        stacked = jnp.concatenate(
            [query * jnp.where(head_lane == h, head_dim**-0.5, 0.0).astype(BF16) for h in range(heads)],
            axis=0,
        )
        scores = (
            lax.dot_general(
                stacked,
                keys[...].reshape(CORES * frames, half),
                (((1,), (1,)), ((), ())),
                preferred_element_type=F32,
            )
            + bias[...]
        )
        shift = jnp.ceil(jnp.max(scores, axis=1, keepdims=True) * 0.25)
        shift = (shift.astype(BF16).astype(F32)) * 4.0
        weights = jnp.exp(scores - shift)
        total = jnp.sum(weights, axis=1, keepdims=True)
        numer = dot(weights.astype(BF16), values[...].reshape(CORES * frames, half))
        high = total.astype(BF16).astype(F32)
        low = total - high
        packed = jnp.zeros((block_rows, half), F32)
        stats = jnp.zeros((block_rows, 128), F32)
        for h in range(heads):
            part = slice(h * block_rows, (h + 1) * block_rows)
            packed = jnp.where(head_lane == h, numer[part], packed)
            begin = h * lane_slot
            stats = jnp.where(stat_lane >= begin, shift[part], stats)
            stats = jnp.where(stat_lane >= begin + lane_slot // 2, high[part], stats)
            stats = jnp.where(stat_lane >= begin + lane_slot * 3 // 4, low[part], stats)
        partial_out[pl.ds(block * group, group), :, :half] = packed.astype(BF16).reshape(
            group, rows, half
        )
        partial_out[pl.ds(block * group, group), :, half:] = stats.astype(BF16).reshape(
            group, rows, 128
        )
        for i in range(group):
            peer = block * group + i

            @pl.when(peer != me)
            def _():
                remote(
                    partial_out.at[peer], partials.at[me], part_send.at[peer], part_recv.at[me], peer
                ).start()

        return carry

    lax.fori_loop(0, blocks, attend, 0)
    partials[me] = partial_out[me]

    for copy in load_rest:
        copy.wait()

    def take_part(step, carry):
        peer = lax.rem(me + step, n)
        remote(
            partial_out.at[peer], partials.at[peer], part_send.at[peer], part_recv.at[peer], peer
        ).wait_recv()
        return carry

    lax.fori_loop(1, n, take_part, 0)

    chips = n // CORES
    stats = dot(partials[:, :, half:].reshape(n * rows, 128), spread[...])
    stats = stats.reshape(chips, CORES, rows, 2 * half)
    numers = partials[:, :, :half].astype(F32).reshape(chips, CORES, rows, half)
    shifts = stats[:, :, :, :half]
    shares = jnp.exp(shifts - jnp.max(shifts, axis=0, keepdims=True))
    attended = jnp.sum(shares * numers, axis=0) / jnp.sum(shares * stats[:, :, :, half:], axis=0)
    attended = jnp.concatenate([attended[i] for i in range(CORES)], axis=1).astype(BF16)

    wide = span[...].astype(F32) + dot(attended, out_w[...])
    mixed = wide.astype(BF16).astype(F32)
    centre = jnp.mean(mixed, axis=1, keepdims=True)
    deviation = mixed - centre
    variance = jnp.mean(deviation * deviation, axis=1, keepdims=True)
    normed = (deviation / jnp.sqrt(variance + 1e-05)).astype(BF16)
    expanded = dot(normed, expand_w[...])
    gated[...] = (expanded[:, :width] * jax.nn.sigmoid(expanded[:, width:])).astype(BF16)

    def halo_copy(side, peer):
        return remote(gated, halo.at[side], halo_send.at[side], halo_recv.at[side], peer)

    @pl.when(me < n - 1)
    def _():
        halo_copy(0, me + 1).start()

    @pl.when(me > 0)
    def _():
        halo_copy(1, me - 1).start()

    padded[rows : 2 * rows] = gated[...].astype(F32)

    @pl.when(me > 0)
    def _():
        halo_copy(0, me - 1).wait_recv()
        padded[:rows] = halo[0].astype(F32)

    @pl.when(me == 0)
    def _():
        padded[:rows] = jnp.zeros((rows, width), F32)

    @pl.when(me < n - 1)
    def _():
        halo_copy(1, me + 1).wait_recv()
        padded[2 * rows :] = halo[1].astype(F32)

    @pl.when(me == n - 1)
    def _():
        padded[2 * rows :] = jnp.zeros((rows, width), F32)

    taps = depth.shape[0]
    first = rows - taps // 2
    conv = jnp.zeros((rows, width), F32)
    for tap in range(taps):
        conv = conv + padded[first + tap : first + tap + rows] * depth[tap : tap + 1]
    normal = conv * norm_scale[...] + norm_shift[...]
    activated = (normal * jax.nn.sigmoid(normal)).astype(BF16)
    out_ref[...] = (mixed + dot(activated, project_w[...])).astype(BF16)

    def finish(step, carry):
        peer = lax.rem(me + step, n)
        query_copy(peer, me, peer).wait_send()
        remote(
            partial_out.at[peer], partials.at[me], part_send.at[peer], part_recv.at[me], peer
        ).wait_send()
        return carry

    lax.fori_loop(1, n, finish, 0)
    key_copy.wait_send()
    mask_copy.wait_send()
    value_copy.wait_send()

    @pl.when(me < n - 1)
    def _():
        halo_copy(0, me + 1).wait_send()

    @pl.when(me > 0)
    def _():
        halo_copy(1, me - 1).wait_send()


def body(
    n,
    span_frames,
    query_rows,
    key_rows,
    context_frames,
    key_mask,
    value_weight,
    out_weight,
    expand_weight,
    depth_weight,
    norm_scale,
    norm_shift,
    project_weight,
):
    rows, width = span_frames.shape
    frames = key_rows.shape[0]
    half = width // CORES
    group = max(1, min(n, 64 // rows))
    vmem = pltpu.VMEM
    dma = pltpu.SemaphoreType.DMA
    args = (
        span_frames,
        query_rows,
        key_rows,
        context_frames,
        key_mask.reshape(1, frames),
        value_weight,
        out_weight,
        expand_weight,
        depth_weight,
        norm_scale.reshape(1, width),
        norm_shift.reshape(1, width),
        project_weight,
    )
    return pl.pallas_call(
        functools.partial(layer_kernel, n, group),
        out_shape=jax.ShapeDtypeStruct((rows, width), BF16),
        in_specs=[pl.BlockSpec(memory_space=pl.ANY)] * len(args),
        out_specs=pl.BlockSpec(memory_space=pltpu.VMEM),
        scratch_shapes=[
            vmem((rows, width), BF16),
            vmem((CORES, rows, half), BF16),
            vmem((CORES, frames, half), BF16),
            vmem((frames, width), BF16),
            vmem((CORES, 1, frames), jnp.int32),
            vmem(value_weight.shape, BF16),
            vmem(out_weight.shape, BF16),
            vmem(expand_weight.shape, BF16),
            vmem(depth_weight.shape, F32),
            vmem((1, width), F32),
            vmem((1, width), F32),
            vmem(project_weight.shape, BF16),
            vmem((frames, half), BF16),
            vmem((CORES, frames, half), BF16),
            vmem((n, rows, half), BF16),
            vmem((n, rows, half + 128), BF16),
            vmem((n, rows, half + 128), BF16),
            vmem((128, 2 * half), BF16),
            vmem((1, CORES * frames), F32),
            vmem((rows, width), BF16),
            vmem((2, rows, width), BF16),
            vmem((3 * rows, width), F32),
            dma((16,)),
            dma((n,)),
            dma((n,)),
            dma((n,)),
            dma((n,)),
            dma((3,)),
            dma((3,)),
            dma((2,)),
            dma((2,)),
        ],
        compiler_params=pltpu.CompilerParams(collective_id=0, has_side_effects=True),
    )(*args)


def solution(mesh):
    rows = P(("groups", "seq"), None)
    in_specs = (rows, rows, rows, rows, P(("groups", "seq"))) + (P(),) * 7
    return jax.shard_map(
        functools.partial(body, mesh.shape["seq"]),
        mesh=mesh,
        in_specs=in_specs,
        out_specs=rows,
        check_vma=False,
    )
```

```python
import functools

import jax
import jax.numpy as jnp
from jax import lax
from jax.experimental import pallas as pl
from jax.experimental.pallas import tpu as pltpu
from jax.sharding import PartitionSpec as P

HEADS = 8
CORES = 2
MESH = pl.DeviceIdType.MESH
F32 = jnp.float32
BF16 = jnp.bfloat16


def dot(a, b):
    return jnp.dot(a, b, preferred_element_type=F32)


def layer_kernel(
    n,
    group,
    span_hbm,
    query_hbm,
    key_hbm,
    context_hbm,
    mask_hbm,
    value_w_hbm,
    out_w_hbm,
    expand_w_hbm,
    depth_hbm,
    scale_hbm,
    shift_hbm,
    project_w_hbm,
    out_ref,
    span,
    own_query,
    keys,
    context,
    mask,
    value_w,
    out_w,
    expand_w,
    depth,
    norm_scale,
    norm_shift,
    project_w,
    value_out,
    values,
    queries,
    partial_out,
    partials,
    spread,
    bias,
    gated,
    halo,
    padded,
    load_sem,
    query_send,
    query_recv,
    part_send,
    part_recv,
    pair_send,
    pair_recv,
    halo_send,
    halo_recv,
):
    me = lax.axis_index("seq")
    core = lax.rem(me, CORES)
    other = 1 - core
    pair = me - core + other
    rows, width = span.shape
    half = width // CORES
    frames = context.shape[0]
    heads = HEADS // CORES
    head_dim = width // HEADS
    block_rows = group * rows
    blocks = n // group
    lane_slot = 128 // heads

    barrier = pltpu.get_barrier_semaphore()

    def greet(step, carry):
        peer = lax.rem(me + step, n)
        pl.semaphore_signal(barrier, inc=1, device_id={"seq": peer}, device_id_type=MESH)
        return carry

    lax.fori_loop(1, n, greet, 0)

    def columns(index):
        return pl.ds(pl.multiple_of(index * half, half), half)

    loads = []

    def load(src, dst):
        copy = pltpu.make_async_copy(src, dst, load_sem.at[len(loads)])
        copy.start()
        loads.append(copy)
        return copy

    load_context = load(context_hbm, context)
    load_value_w = load(value_w_hbm, value_w)
    load_query = [load(query_hbm.at[:, i * half : (i + 1) * half], own_query.at[i]) for i in range(CORES)]
    load_mask = load(mask_hbm, mask.at[core])
    load_keys = load(key_hbm.at[:, columns(core)], keys.at[core])
    load_rest = [
        load(src, dst)
        for src, dst in (
            (span_hbm, span),
            (out_w_hbm, out_w),
            (expand_w_hbm, expand_w),
            (depth_hbm, depth),
            (scale_hbm, norm_scale),
            (shift_hbm, norm_shift),
            (project_w_hbm, project_w),
        )
    ]

    load_context.wait()
    load_value_w.wait()
    value_out[...] = dot(context[...], value_w[:, columns(other)]).astype(BF16)
    for copy in load_query:
        copy.wait()
    load_mask.wait()

    values[core] = dot(context[...], value_w[:, columns(core)]).astype(BF16)
    slot_row = lax.broadcasted_iota(jnp.int32, (128, 2 * half), 0)
    slot_col = lax.broadcasted_iota(jnp.int32, (128, 2 * half), 1)
    slot_head = lax.rem(slot_col, half) // head_dim * lane_slot
    shift_pick = jnp.logical_and(slot_col < half, slot_row == slot_head)
    total_pick = jnp.logical_and(
        slot_col >= half,
        jnp.logical_or(
            slot_row == slot_head + lane_slot // 2, slot_row == slot_head + lane_slot * 3 // 4
        ),
    )
    spread[...] = jnp.where(jnp.logical_or(shift_pick, total_pick), 1.0, 0.0).astype(BF16)

    pl.semaphore_wait(barrier, n - 1)

    def remote(src, dst, send, recv, peer):
        return pltpu.make_async_remote_copy(
            src_ref=src,
            dst_ref=dst,
            send_sem=send,
            recv_sem=recv,
            device_id={"seq": peer},
            device_id_type=MESH,
        )

    def query_copy(peer, slot, sem_index):
        return remote(
            own_query.at[lax.rem(peer, CORES)],
            queries.at[slot],
            query_send.at[sem_index],
            query_recv.at[slot],
            peer,
        )

    key_copy = remote(
        key_hbm.at[:, columns(other)], keys.at[core], pair_send.at[0], pair_recv.at[0], pair
    )
    mask_copy = remote(mask.at[core], mask.at[core], pair_send.at[1], pair_recv.at[1], pair)
    value_copy = remote(value_out, values.at[core], pair_send.at[2], pair_recv.at[2], pair)
    key_copy.start()
    mask_copy.start()

    def send_query(step, carry):
        peer = lax.rem(me + step, n)
        query_copy(peer, me, peer).start()
        return carry

    lax.fori_loop(1, n, send_query, 0)
    value_copy.start()

    queries[me] = own_query[core]
    load_keys.wait()
    remote(keys.at[other], keys.at[other], pair_send.at[0], pair_recv.at[0], pair).wait_recv()
    remote(mask.at[other], mask.at[other], pair_send.at[1], pair_recv.at[1], pair).wait_recv()
    for i in range(CORES):
        bias[:, i * frames : (i + 1) * frames] = jnp.where(mask[i] > 0, 0.0, -1e30)
    remote(values.at[other], values.at[other], pair_send.at[2], pair_recv.at[2], pair).wait_recv()

    head_lane = lax.broadcasted_iota(jnp.int32, (1, half), 1) // head_dim
    stat_lane = lax.broadcasted_iota(jnp.int32, (1, 128), 1)
    first_block = me // group
    heading = 1 - 2 * (2 * first_block // blocks)

    def attend(step, carry):
        block = lax.rem(first_block + heading * step + blocks, blocks)
        for i in range(group):
            source = block * group + i

            @pl.when(source != me)
            def _():
                query_copy(pair, source, source).wait_recv()

        query = queries[pl.ds(block * group, group)].reshape(block_rows, half)
        stacked = jnp.concatenate(
            [query * jnp.where(head_lane == h, head_dim**-0.5, 0.0).astype(BF16) for h in range(heads)],
            axis=0,
        )
        scores = (
            lax.dot_general(
                stacked,
                keys[...].reshape(CORES * frames, half),
                (((1,), (1,)), ((), ())),
                preferred_element_type=F32,
            )
            + bias[...]
        )
        shift = jnp.ceil(jnp.max(scores, axis=1, keepdims=True) * 0.25)
        shift = (shift.astype(BF16).astype(F32)) * 4.0
        weights = jnp.exp(scores - shift)
        total = jnp.sum(weights, axis=1, keepdims=True)
        numer = dot(weights.astype(BF16), values[...].reshape(CORES * frames, half))
        high = total.astype(BF16).astype(F32)
        low = total - high
        packed = jnp.zeros((block_rows, half), F32)
        stats = jnp.zeros((block_rows, 128), F32)
        for h in range(heads):
            part = slice(h * block_rows, (h + 1) * block_rows)
            packed = jnp.where(head_lane == h, numer[part], packed)
            begin = h * lane_slot
            stats = jnp.where(stat_lane >= begin, shift[part], stats)
            stats = jnp.where(stat_lane >= begin + lane_slot // 2, high[part], stats)
            stats = jnp.where(stat_lane >= begin + lane_slot * 3 // 4, low[part], stats)
        partial_out[pl.ds(block * group, group), :, :half] = packed.astype(BF16).reshape(
            group, rows, half
        )
        partial_out[pl.ds(block * group, group), :, half:] = stats.astype(BF16).reshape(
            group, rows, 128
        )
        for i in range(group):
            peer = block * group + i

            @pl.when(peer != me)
            def _():
                remote(
                    partial_out.at[peer], partials.at[me], part_send.at[peer], part_recv.at[me], peer
                ).start()

        return carry

    lax.fori_loop(0, blocks, attend, 0)
    partials[me] = partial_out[me]

    for copy in load_rest:
        copy.wait()

    def take_part(step, carry):
        peer = lax.rem(me + step, n)
        remote(
            partial_out.at[peer], partials.at[peer], part_send.at[peer], part_recv.at[peer], peer
        ).wait_recv()
        return carry

    lax.fori_loop(1, n, take_part, 0)

    chips = n // CORES
    stats = dot(partials[:, :, half:].reshape(n * rows, 128), spread[...])
    stats = stats.reshape(chips, CORES, rows, 2 * half)
    numers = partials[:, :, :half].astype(F32).reshape(chips, CORES, rows, half)
    shifts = stats[:, :, :, :half]
    shares = jnp.exp(shifts - jnp.max(shifts, axis=0, keepdims=True))
    attended = jnp.sum(shares * numers, axis=0) / jnp.sum(shares * stats[:, :, :, half:], axis=0)
    attended = jnp.concatenate([attended[i] for i in range(CORES)], axis=1).astype(BF16)

    wide = span[...].astype(F32) + dot(attended, out_w[...])
    mixed = wide.astype(BF16).astype(F32)
    centre = jnp.mean(mixed, axis=1, keepdims=True)
    deviation = mixed - centre
    variance = jnp.mean(deviation * deviation, axis=1, keepdims=True)
    normed = (deviation / jnp.sqrt(variance + 1e-05)).astype(BF16)
    expanded = dot(normed, expand_w[...])
    gated[...] = (expanded[:, :width] * jax.nn.sigmoid(expanded[:, width:])).astype(BF16)

    def halo_copy(side, peer):
        return remote(gated, halo.at[side], halo_send.at[side], halo_recv.at[side], peer)

    @pl.when(me < n - 1)
    def _():
        halo_copy(0, me + 1).start()

    @pl.when(me > 0)
    def _():
        halo_copy(1, me - 1).start()

    padded[rows : 2 * rows] = gated[...].astype(F32)

    @pl.when(me > 0)
    def _():
        halo_copy(0, me - 1).wait_recv()
        padded[:rows] = halo[0].astype(F32)

    @pl.when(me == 0)
    def _():
        padded[:rows] = jnp.zeros((rows, width), F32)

    @pl.when(me < n - 1)
    def _():
        halo_copy(1, me + 1).wait_recv()
        padded[2 * rows :] = halo[1].astype(F32)

    @pl.when(me == n - 1)
    def _():
        padded[2 * rows :] = jnp.zeros((rows, width), F32)

    taps = depth.shape[0]
    first = rows - taps // 2
    conv = jnp.zeros((rows, width), F32)
    for tap in range(taps):
        conv = conv + padded[first + tap : first + tap + rows] * depth[tap : tap + 1]
    normal = conv * norm_scale[...] + norm_shift[...]
    activated = (normal * jax.nn.sigmoid(normal)).astype(BF16)
    out_ref[...] = (mixed + dot(activated, project_w[...])).astype(BF16)

    def finish(step, carry):
        peer = lax.rem(me + step, n)
        query_copy(peer, me, peer).wait_send()
        remote(
            partial_out.at[peer], partials.at[me], part_send.at[peer], part_recv.at[me], peer
        ).wait_send()
        return carry

    lax.fori_loop(1, n, finish, 0)
    key_copy.wait_send()
    mask_copy.wait_send()
    value_copy.wait_send()

    @pl.when(me < n - 1)
    def _():
        halo_copy(0, me + 1).wait_send()

    @pl.when(me > 0)
    def _():
        halo_copy(1, me - 1).wait_send()


def body(
    n,
    span_frames,
    query_rows,
    key_rows,
    context_frames,
    key_mask,
    value_weight,
    out_weight,
    expand_weight,
    depth_weight,
    norm_scale,
    norm_shift,
    project_weight,
):
    rows, width = span_frames.shape
    frames = key_rows.shape[0]
    half = width // CORES
    group = max(1, min(n, 64 // rows))
    vmem = pltpu.VMEM
    dma = pltpu.SemaphoreType.DMA
    args = (
        span_frames,
        query_rows,
        key_rows,
        context_frames,
        key_mask.reshape(1, frames),
        value_weight,
        out_weight,
        expand_weight,
        depth_weight,
        norm_scale.reshape(1, width),
        norm_shift.reshape(1, width),
        project_weight,
    )
    return pl.pallas_call(
        functools.partial(layer_kernel, n, group),
        out_shape=pltpu.VMEM((rows, width), BF16),
        in_specs=[pl.BlockSpec(memory_space=pl.ANY)] * len(args),
        out_specs=pl.BlockSpec(memory_space=pltpu.VMEM),
        scratch_shapes=[
            vmem((rows, width), BF16),
            vmem((CORES, rows, half), BF16),
            vmem((CORES, frames, half), BF16),
            vmem((frames, width), BF16),
            vmem((CORES, 1, frames), jnp.int32),
            vmem(value_weight.shape, BF16),
            vmem(out_weight.shape, BF16),
            vmem(expand_weight.shape, BF16),
            vmem(depth_weight.shape, F32),
            vmem((1, width), F32),
            vmem((1, width), F32),
            vmem(project_weight.shape, BF16),
            vmem((frames, half), BF16),
            vmem((CORES, frames, half), BF16),
            vmem((n, rows, half), BF16),
            vmem((n, rows, half + 128), BF16),
            vmem((n, rows, half + 128), BF16),
            vmem((128, 2 * half), BF16),
            vmem((1, CORES * frames), F32),
            vmem((rows, width), BF16),
            vmem((2, rows, width), BF16),
            vmem((3 * rows, width), F32),
            dma((16,)),
            dma((n,)),
            dma((n,)),
            dma((n,)),
            dma((n,)),
            dma((3,)),
            dma((3,)),
            dma((2,)),
            dma((2,)),
        ],
        compiler_params=pltpu.CompilerParams(collective_id=0, has_side_effects=True),
    )(*args)


def solution(mesh):
    rows = P(("groups", "seq"), None)
    in_specs = (rows, rows, rows, rows, P(("groups", "seq"))) + (P(),) * 7
    return jax.shard_map(
        functools.partial(body, mesh.shape["seq"]),
        mesh=mesh,
        in_specs=in_specs,
        out_specs=rows,
        check_vma=False,
    )
```

```python
import functools

import jax
import jax.numpy as jnp
from jax import lax
from jax.experimental import pallas as pl
from jax.experimental.pallas import tpu as pltpu
from jax.sharding import PartitionSpec as P

HEADS = 8
CORES = 2
MESH = pl.DeviceIdType.MESH
F32 = jnp.float32
BF16 = jnp.bfloat16


def dot(a, b):
    return jnp.dot(a, b, preferred_element_type=F32)


def layer_kernel(
    n,
    group,
    span_hbm,
    query_hbm,
    key_hbm,
    context_hbm,
    mask_hbm,
    value_w_hbm,
    out_w_hbm,
    expand_w_hbm,
    depth_hbm,
    scale_hbm,
    shift_hbm,
    project_w_hbm,
    out_ref,
    span,
    own_query,
    keys,
    context,
    mask,
    value_w,
    out_w,
    expand_w,
    depth,
    norm_scale,
    norm_shift,
    project_w,
    value_out,
    values,
    queries,
    partial_out,
    partials,
    stat_out,
    stat_in,
    spread,
    bias,
    gated,
    halo,
    padded,
    load_sem,
    query_send,
    query_recv,
    part_send,
    part_recv,
    stat_send,
    stat_recv,
    pair_send,
    pair_recv,
    halo_send,
    halo_recv,
):
    me = lax.axis_index("seq")
    core = lax.rem(me, CORES)
    other = 1 - core
    pair = me - core + other
    rows, width = span.shape
    half = width // CORES
    frames = context.shape[0]
    heads = HEADS // CORES
    head_dim = width // HEADS
    block_rows = group * rows
    blocks = n // group

    barrier = pltpu.get_barrier_semaphore()

    def greet(step, carry):
        peer = lax.rem(me + step, n)
        pl.semaphore_signal(barrier, inc=1, device_id={"seq": peer}, device_id_type=MESH)
        return carry

    lax.fori_loop(1, n, greet, 0)

    def columns(index):
        return pl.ds(pl.multiple_of(index * half, half), half)

    loads = []

    def load(src, dst):
        copy = pltpu.make_async_copy(src, dst, load_sem.at[len(loads)])
        copy.start()
        loads.append(copy)
        return copy

    load_context = load(context_hbm, context)
    load_value_w = load(value_w_hbm, value_w)
    load_query = [load(query_hbm.at[:, i * half : (i + 1) * half], own_query.at[i]) for i in range(CORES)]
    load_mask = load(mask_hbm, mask.at[core])
    load_keys = load(key_hbm.at[:, columns(core)], keys.at[core])
    load_rest = [
        load(src, dst)
        for src, dst in (
            (span_hbm, span),
            (out_w_hbm, out_w),
            (expand_w_hbm, expand_w),
            (depth_hbm, depth),
            (scale_hbm, norm_scale),
            (shift_hbm, norm_shift),
            (project_w_hbm, project_w),
        )
    ]

    load_context.wait()
    load_value_w.wait()
    value_out[...] = dot(context[...], value_w[:, columns(other)]).astype(BF16)
    for copy in load_query:
        copy.wait()
    load_mask.wait()

    values[core] = dot(context[...], value_w[:, columns(core)]).astype(BF16)
    fields = 2 * heads
    stat_width = stat_out.shape[-1]
    slot = lax.rem(lax.broadcasted_iota(jnp.int32, (stat_width, 2 * half), 0), fields)
    target = lax.broadcasted_iota(jnp.int32, (stat_width, 2 * half), 1)
    wanted = lax.rem(target, half) // head_dim * 2 + target // half
    spread[...] = jnp.where(slot == wanted, 1.0, 0.0).astype(BF16)
    field = lax.rem(lax.broadcasted_iota(jnp.int32, (1, stat_width), 1), fields)
    own_row = (
        lax.broadcasted_iota(jnp.int32, (1, rows, stat_width), 2) // fields
        == lax.broadcasted_iota(jnp.int32, (1, rows, stat_width), 1)
    )

    pl.semaphore_wait(barrier, n - 1)

    def remote(src, dst, send, recv, peer):
        return pltpu.make_async_remote_copy(
            src_ref=src,
            dst_ref=dst,
            send_sem=send,
            recv_sem=recv,
            device_id={"seq": peer},
            device_id_type=MESH,
        )

    def query_copy(peer, slot, sem_index):
        return remote(
            own_query.at[lax.rem(peer, CORES)],
            queries.at[slot],
            query_send.at[sem_index],
            query_recv.at[slot],
            peer,
        )

    def part_copies(peer, place):
        return (
            remote(
                stat_out.at[peer], stat_in.at[place], stat_send.at[peer], stat_recv.at[place], peer
            ),
            remote(
                partial_out.at[peer], partials.at[place], part_send.at[peer], part_recv.at[place], peer
            ),
        )

    key_copy = remote(
        key_hbm.at[:, columns(other)], keys.at[core], pair_send.at[0], pair_recv.at[0], pair
    )
    mask_copy = remote(mask.at[core], mask.at[core], pair_send.at[1], pair_recv.at[1], pair)
    value_copy = remote(value_out, values.at[core], pair_send.at[2], pair_recv.at[2], pair)
    key_copy.start()
    mask_copy.start()

    def send_query(step, carry):
        peer = lax.rem(me + step, n)
        query_copy(peer, me, peer).start()
        return carry

    lax.fori_loop(1, n, send_query, 0)
    value_copy.start()

    queries[me] = own_query[core]
    load_keys.wait()
    remote(keys.at[other], keys.at[other], pair_send.at[0], pair_recv.at[0], pair).wait_recv()
    remote(mask.at[other], mask.at[other], pair_send.at[1], pair_recv.at[1], pair).wait_recv()
    for i in range(CORES):
        bias[:, i * frames : (i + 1) * frames] = jnp.where(mask[i] > 0, 0.0, -1e30)
    remote(values.at[other], values.at[other], pair_send.at[2], pair_recv.at[2], pair).wait_recv()

    head_lane = lax.broadcasted_iota(jnp.int32, (1, half), 1) // head_dim
    first_block = me // group
    heading = 1 - 2 * (2 * first_block // blocks)

    def attend(step, carry):
        block = lax.rem(first_block + heading * step + blocks, blocks)
        for i in range(group):
            source = block * group + i

            @pl.when(source != me)
            def _():
                query_copy(pair, source, source).wait_recv()

        query = queries[pl.ds(block * group, group)].reshape(block_rows, half)
        stacked = jnp.concatenate(
            [query * jnp.where(head_lane == h, head_dim**-0.5, 0.0).astype(BF16) for h in range(heads)],
            axis=0,
        )
        scores = (
            lax.dot_general(
                stacked,
                keys[...].reshape(CORES * frames, half),
                (((1,), (1,)), ((), ())),
                preferred_element_type=F32,
            )
            + bias[...]
        )
        shift = jnp.ceil(jnp.max(scores, axis=1, keepdims=True) * 0.25)
        shift = (shift.astype(BF16).astype(F32)) * 4.0
        weights = jnp.exp(scores - shift)
        total = jnp.sum(weights, axis=1, keepdims=True)
        numer = dot(weights.astype(BF16), values[...].reshape(CORES * frames, half))
        packed = jnp.zeros((block_rows, half), F32)
        stats = jnp.zeros((block_rows, stat_width), F32)
        for h in range(heads):
            part = slice(h * block_rows, (h + 1) * block_rows)
            packed = jnp.where(head_lane == h, numer[part], packed)
            stats = jnp.where(field == 2 * h, shift[part], stats)
            stats = jnp.where(field == 2 * h + 1, total[part], stats)
        stats = jnp.where(own_row, stats.reshape(group, rows, stat_width), 0.0)
        stat_out[pl.ds(block * group, group)] = jnp.sum(stats, axis=1, keepdims=True)
        partial_out[pl.ds(block * group, group)] = packed.astype(BF16).reshape(group, rows, half)
        for i in range(group):
            peer = block * group + i

            @pl.when(peer != me)
            def _():
                for copy in part_copies(peer, me):
                    copy.start()

        return carry

    lax.fori_loop(0, blocks, attend, 0)
    partials[me] = partial_out[me]
    stat_in[me] = stat_out[me]

    for copy in load_rest:
        copy.wait()

    def take_part(step, carry):
        peer = lax.rem(me + step, n)
        for copy in part_copies(peer, peer):
            copy.wait_recv()
        return carry

    lax.fori_loop(1, n, take_part, 0)

    chips = n // CORES
    stats = jnp.where(own_row, stat_in[...], 0.0).reshape(n * rows, stat_width)
    high = stats.astype(BF16)
    low = (stats - high.astype(F32)).astype(BF16)
    stats = dot(high, spread[...]) + dot(low, spread[...])
    stats = stats.reshape(chips, CORES, rows, 2 * half)
    numers = partials[...].astype(F32).reshape(chips, CORES, rows, half)
    shifts = stats[:, :, :, :half]
    shares = jnp.exp(shifts - jnp.max(shifts, axis=0, keepdims=True))
    attended = jnp.sum(shares * numers, axis=0) / jnp.sum(shares * stats[:, :, :, half:], axis=0)
    attended = jnp.concatenate([attended[i] for i in range(CORES)], axis=1).astype(BF16)

    wide = span[...].astype(F32) + dot(attended, out_w[...])
    mixed = wide.astype(BF16).astype(F32)
    centre = jnp.mean(mixed, axis=1, keepdims=True)
    deviation = mixed - centre
    variance = jnp.mean(deviation * deviation, axis=1, keepdims=True)
    normed = (deviation / jnp.sqrt(variance + 1e-05)).astype(BF16)
    expanded = dot(normed, expand_w[...])
    gated[...] = (expanded[:, :width] * jax.nn.sigmoid(expanded[:, width:])).astype(BF16)

    def halo_copy(side, peer):
        return remote(gated, halo.at[side], halo_send.at[side], halo_recv.at[side], peer)

    @pl.when(me < n - 1)
    def _():
        halo_copy(0, me + 1).start()

    @pl.when(me > 0)
    def _():
        halo_copy(1, me - 1).start()

    padded[rows : 2 * rows] = gated[...].astype(F32)

    @pl.when(me > 0)
    def _():
        halo_copy(0, me - 1).wait_recv()
        padded[:rows] = halo[0].astype(F32)

    @pl.when(me == 0)
    def _():
        padded[:rows] = jnp.zeros((rows, width), F32)

    @pl.when(me < n - 1)
    def _():
        halo_copy(1, me + 1).wait_recv()
        padded[2 * rows :] = halo[1].astype(F32)

    @pl.when(me == n - 1)
    def _():
        padded[2 * rows :] = jnp.zeros((rows, width), F32)

    taps = depth.shape[0]
    first = rows - taps // 2
    conv = jnp.zeros((rows, width), F32)
    for tap in range(taps):
        conv = conv + padded[first + tap : first + tap + rows] * depth[tap : tap + 1]
    normal = conv * norm_scale[...] + norm_shift[...]
    activated = (normal * jax.nn.sigmoid(normal)).astype(BF16)
    out_ref[...] = (mixed + dot(activated, project_w[...])).astype(BF16)

    def finish(step, carry):
        peer = lax.rem(me + step, n)
        query_copy(peer, me, peer).wait_send()
        for copy in part_copies(peer, me):
            copy.wait_send()
        return carry

    lax.fori_loop(1, n, finish, 0)
    key_copy.wait_send()
    mask_copy.wait_send()
    value_copy.wait_send()

    @pl.when(me < n - 1)
    def _():
        halo_copy(0, me + 1).wait_send()

    @pl.when(me > 0)
    def _():
        halo_copy(1, me - 1).wait_send()


def body(
    n,
    span_frames,
    query_rows,
    key_rows,
    context_frames,
    key_mask,
    value_weight,
    out_weight,
    expand_weight,
    depth_weight,
    norm_scale,
    norm_shift,
    project_weight,
):
    rows, width = span_frames.shape
    frames = key_rows.shape[0]
    half = width // CORES
    group = max(1, min(n, 64 // rows))
    stat_width = rows * 2 * (HEADS // CORES)
    vmem = pltpu.VMEM
    dma = pltpu.SemaphoreType.DMA
    args = (
        span_frames,
        query_rows,
        key_rows,
        context_frames,
        key_mask.reshape(1, frames),
        value_weight,
        out_weight,
        expand_weight,
        depth_weight,
        norm_scale.reshape(1, width),
        norm_shift.reshape(1, width),
        project_weight,
    )
    return pl.pallas_call(
        functools.partial(layer_kernel, n, group),
        out_shape=pltpu.VMEM((rows, width), BF16),
        in_specs=[pl.BlockSpec(memory_space=pl.ANY)] * len(args),
        out_specs=pl.BlockSpec(memory_space=pltpu.VMEM),
        scratch_shapes=[
            vmem((rows, width), BF16),
            vmem((CORES, rows, half), BF16),
            vmem((CORES, frames, half), BF16),
            vmem((frames, width), BF16),
            vmem((CORES, 1, frames), jnp.int32),
            vmem(value_weight.shape, BF16),
            vmem(out_weight.shape, BF16),
            vmem(expand_weight.shape, BF16),
            vmem(depth_weight.shape, F32),
            vmem((1, width), F32),
            vmem((1, width), F32),
            vmem(project_weight.shape, BF16),
            vmem((frames, half), BF16),
            vmem((CORES, frames, half), BF16),
            vmem((n, rows, half), BF16),
            vmem((n, rows, half), BF16),
            vmem((n, rows, half), BF16),
            vmem((n, 1, stat_width), F32),
            vmem((n, 1, stat_width), F32),
            vmem((stat_width, 2 * half), BF16),
            vmem((1, CORES * frames), F32),
            vmem((rows, width), BF16),
            vmem((2, rows, width), BF16),
            vmem((3 * rows, width), F32),
            dma((16,)),
            dma((n,)),
            dma((n,)),
            dma((n,)),
            dma((n,)),
            dma((n,)),
            dma((n,)),
            dma((3,)),
            dma((3,)),
            dma((2,)),
            dma((2,)),
        ],
        compiler_params=pltpu.CompilerParams(collective_id=0, has_side_effects=True),
    )(*args)


def solution(mesh):
    rows = P(("groups", "seq"), None)
    in_specs = (rows, rows, rows, rows, P(("groups", "seq"))) + (P(),) * 7
    return jax.shard_map(
        functools.partial(body, mesh.shape["seq"]),
        mesh=mesh,
        in_specs=in_specs,
        out_specs=rows,
        check_vma=False,
    )
```

```python
import functools

import jax
import jax.numpy as jnp
from jax import lax
from jax.experimental import pallas as pl
from jax.experimental.pallas import tpu as pltpu
from jax.sharding import PartitionSpec as P

HEADS = 8
CORES = 2
MESH = pl.DeviceIdType.MESH
F32 = jnp.float32
BF16 = jnp.bfloat16


def dot(a, b):
    return jnp.dot(a, b, preferred_element_type=F32)


def layer_kernel(
    n,
    group,
    span_hbm,
    query_hbm,
    key_hbm,
    context_hbm,
    mask_hbm,
    value_w_hbm,
    out_w_hbm,
    expand_w_hbm,
    depth_hbm,
    scale_hbm,
    shift_hbm,
    project_w_hbm,
    out_ref,
    span,
    own_query,
    keys,
    context,
    mask,
    value_w,
    out_w,
    expand_w,
    depth,
    norm_scale,
    norm_shift,
    project_w,
    value_out,
    values,
    queries,
    partial_out,
    partials,
    stat_out,
    stat_in,
    spread,
    bias,
    gated,
    halo,
    padded,
    load_sem,
    query_send,
    query_recv,
    part_send,
    part_recv,
    stat_send,
    stat_recv,
    pair_send,
    pair_recv,
    halo_send,
    halo_recv,
):
    me = lax.axis_index("seq")
    core = lax.rem(me, CORES)
    other = 1 - core
    pair = me - core + other
    rows, width = span.shape
    half = width // CORES
    frames = context.shape[0]
    heads = HEADS // CORES
    head_dim = width // HEADS
    block_rows = group * rows
    blocks = n // group
    unroll = n <= 32

    barrier = pltpu.get_barrier_semaphore()

    def greet(step, carry):
        peer = lax.rem(me + step, n)
        pl.semaphore_signal(barrier, inc=1, device_id={"seq": peer}, device_id_type=MESH)
        return carry

    lax.fori_loop(1, n, greet, 0, unroll=unroll)

    def columns(index):
        return pl.ds(pl.multiple_of(index * half, half), half)

    loads = []

    def load(src, dst):
        copy = pltpu.make_async_copy(src, dst, load_sem.at[len(loads)])
        copy.start()
        loads.append(copy)
        return copy

    load_context = load(context_hbm, context)
    load_value_w = load(value_w_hbm, value_w)
    load_query = [load(query_hbm.at[:, i * half : (i + 1) * half], own_query.at[i]) for i in range(CORES)]
    load_mask = load(mask_hbm, mask.at[core])
    load_keys = load(key_hbm.at[:, columns(core)], keys.at[core])
    load_rest = [
        load(src, dst)
        for src, dst in (
            (span_hbm, span),
            (out_w_hbm, out_w),
            (expand_w_hbm, expand_w),
            (depth_hbm, depth),
            (scale_hbm, norm_scale),
            (shift_hbm, norm_shift),
            (project_w_hbm, project_w),
        )
    ]

    load_context.wait()
    load_value_w.wait()
    value_out[...] = dot(context[...], value_w[:, columns(other)]).astype(BF16)
    for copy in load_query:
        copy.wait()
    load_mask.wait()

    values[core] = dot(context[...], value_w[:, columns(core)]).astype(BF16)
    fields = 2 * heads
    stat_width = stat_out.shape[-1]
    slot = lax.rem(lax.broadcasted_iota(jnp.int32, (stat_width, 2 * half), 0), fields)
    target = lax.broadcasted_iota(jnp.int32, (stat_width, 2 * half), 1)
    wanted = lax.rem(target, half) // head_dim * 2 + target // half
    spread[...] = jnp.where(slot == wanted, 1.0, 0.0).astype(BF16)
    field = lax.rem(lax.broadcasted_iota(jnp.int32, (1, stat_width), 1), fields)
    own_row = (
        lax.broadcasted_iota(jnp.int32, (1, rows, stat_width), 2) // fields
        == lax.broadcasted_iota(jnp.int32, (1, rows, stat_width), 1)
    )

    pl.semaphore_wait(barrier, n - 1)

    def remote(src, dst, send, recv, peer):
        return pltpu.make_async_remote_copy(
            src_ref=src,
            dst_ref=dst,
            send_sem=send,
            recv_sem=recv,
            device_id={"seq": peer},
            device_id_type=MESH,
        )

    def query_copy(peer, slot, sem_index):
        return remote(
            own_query.at[lax.rem(peer, CORES)],
            queries.at[slot],
            query_send.at[sem_index],
            query_recv.at[slot],
            peer,
        )

    def part_copies(peer, place):
        return (
            remote(
                stat_out.at[peer], stat_in.at[place], stat_send.at[peer], stat_recv.at[place], peer
            ),
            remote(
                partial_out.at[peer], partials.at[place], part_send.at[peer], part_recv.at[place], peer
            ),
        )

    key_copy = remote(
        key_hbm.at[:, columns(other)], keys.at[core], pair_send.at[0], pair_recv.at[0], pair
    )
    mask_copy = remote(mask.at[core], mask.at[core], pair_send.at[1], pair_recv.at[1], pair)
    value_copy = remote(value_out, values.at[core], pair_send.at[2], pair_recv.at[2], pair)
    key_copy.start()
    mask_copy.start()

    first_block = me // group
    heading = 1 - 2 * (2 * first_block // blocks)

    def send_query(step, carry):
        spot = step
        peer = lax.rem(first_block + heading * (spot // group) + blocks, blocks) * group + lax.rem(me + lax.rem(spot, group), group)

        @pl.when(peer != me)
        def _():
            query_copy(peer, me, peer).start()

        return carry

    lax.fori_loop(0, n, send_query, 0, unroll=unroll)
    value_copy.start()

    queries[me] = own_query[core]
    load_keys.wait()
    remote(keys.at[other], keys.at[other], pair_send.at[0], pair_recv.at[0], pair).wait_recv()
    remote(mask.at[other], mask.at[other], pair_send.at[1], pair_recv.at[1], pair).wait_recv()
    for i in range(CORES):
        bias[:, i * frames : (i + 1) * frames] = jnp.where(mask[i] > 0, 0.0, -1e30)
    remote(values.at[other], values.at[other], pair_send.at[2], pair_recv.at[2], pair).wait_recv()

    head_lane = lax.broadcasted_iota(jnp.int32, (1, half), 1) // head_dim

    def attend(step, carry):
        block = lax.rem(first_block + heading * step + blocks, blocks)
        for i in range(group):
            source = block * group + i

            @pl.when(source != me)
            def _():
                query_copy(pair, source, source).wait_recv()

        query = queries[pl.ds(block * group, group)].reshape(block_rows, half)
        stacked = jnp.concatenate(
            [query * jnp.where(head_lane == h, head_dim**-0.5, 0.0).astype(BF16) for h in range(heads)],
            axis=0,
        )
        scores = (
            lax.dot_general(
                stacked,
                keys[...].reshape(CORES * frames, half),
                (((1,), (1,)), ((), ())),
                preferred_element_type=F32,
            )
            + bias[...]
        )
        shift = jnp.ceil(jnp.max(scores, axis=1, keepdims=True) * 0.25)
        shift = (shift.astype(BF16).astype(F32)) * 4.0
        weights = jnp.exp(scores - shift)
        total = jnp.sum(weights, axis=1, keepdims=True)
        numer = dot(weights.astype(BF16), values[...].reshape(CORES * frames, half))
        packed = jnp.zeros((block_rows, half), F32)
        stats = jnp.zeros((block_rows, stat_width), F32)
        for h in range(heads):
            part = slice(h * block_rows, (h + 1) * block_rows)
            packed = jnp.where(head_lane == h, numer[part], packed)
            stats = jnp.where(field == 2 * h, shift[part], stats)
            stats = jnp.where(field == 2 * h + 1, total[part], stats)
        stats = jnp.where(own_row, stats.reshape(group, rows, stat_width), 0.0)
        stat_out[pl.ds(block * group, group)] = jnp.sum(stats, axis=1, keepdims=True)
        partial_out[pl.ds(block * group, group)] = packed.astype(BF16).reshape(group, rows, half)
        for i in range(group):
            peer = block * group + i

            @pl.when(peer != me)
            def _():
                for copy in part_copies(peer, me):
                    copy.start()

        return carry

    lax.fori_loop(0, blocks, attend, 0, unroll=unroll)
    partials[me] = partial_out[me]
    stat_in[me] = stat_out[me]

    for copy in load_rest:
        copy.wait()

    def take_part(step, carry):
        peer = lax.rem(me + step, n)
        for copy in part_copies(peer, peer):
            copy.wait_recv()
        return carry

    lax.fori_loop(1, n, take_part, 0, unroll=unroll)

    chips = n // CORES
    stats = jnp.where(own_row, stat_in[...], 0.0).reshape(n * rows, stat_width)
    high = stats.astype(BF16)
    low = (stats - high.astype(F32)).astype(BF16)
    stats = dot(high, spread[...]) + dot(low, spread[...])
    stats = stats.reshape(chips, CORES, rows, 2 * half)
    numers = partials[...].astype(F32).reshape(chips, CORES, rows, half)
    shifts = stats[:, :, :, :half]
    shares = jnp.exp(shifts - jnp.max(shifts, axis=0, keepdims=True))
    attended = jnp.sum(shares * numers, axis=0) / jnp.sum(shares * stats[:, :, :, half:], axis=0)
    attended = jnp.concatenate([attended[i] for i in range(CORES)], axis=1).astype(BF16)

    wide = span[...].astype(F32) + dot(attended, out_w[...])
    mixed = wide.astype(BF16).astype(F32)
    centre = jnp.mean(mixed, axis=1, keepdims=True)
    deviation = mixed - centre
    variance = jnp.mean(deviation * deviation, axis=1, keepdims=True)
    normed = (deviation / jnp.sqrt(variance + 1e-05)).astype(BF16)
    expanded = dot(normed, expand_w[...])
    gated[...] = (expanded[:, :width] * jax.nn.sigmoid(expanded[:, width:])).astype(BF16)

    def halo_copy(side, peer):
        return remote(gated, halo.at[side], halo_send.at[side], halo_recv.at[side], peer)

    @pl.when(me < n - 1)
    def _():
        halo_copy(0, me + 1).start()

    @pl.when(me > 0)
    def _():
        halo_copy(1, me - 1).start()

    padded[rows : 2 * rows] = gated[...].astype(F32)

    @pl.when(me > 0)
    def _():
        halo_copy(0, me - 1).wait_recv()
        padded[:rows] = halo[0].astype(F32)

    @pl.when(me == 0)
    def _():
        padded[:rows] = jnp.zeros((rows, width), F32)

    @pl.when(me < n - 1)
    def _():
        halo_copy(1, me + 1).wait_recv()
        padded[2 * rows :] = halo[1].astype(F32)

    @pl.when(me == n - 1)
    def _():
        padded[2 * rows :] = jnp.zeros((rows, width), F32)

    taps = depth.shape[0]
    first = rows - taps // 2
    conv = jnp.zeros((rows, width), F32)
    for tap in range(taps):
        conv = conv + padded[first + tap : first + tap + rows] * depth[tap : tap + 1]
    normal = conv * norm_scale[...] + norm_shift[...]
    activated = (normal * jax.nn.sigmoid(normal)).astype(BF16)
    out_ref[...] = (mixed + dot(activated, project_w[...])).astype(BF16)

    def finish(step, carry):
        peer = lax.rem(me + step, n)
        query_copy(peer, me, peer).wait_send()
        for copy in part_copies(peer, me):
            copy.wait_send()
        return carry

    lax.fori_loop(1, n, finish, 0, unroll=unroll)
    key_copy.wait_send()
    mask_copy.wait_send()
    value_copy.wait_send()

    @pl.when(me < n - 1)
    def _():
        halo_copy(0, me + 1).wait_send()

    @pl.when(me > 0)
    def _():
        halo_copy(1, me - 1).wait_send()


def body(
    n,
    span_frames,
    query_rows,
    key_rows,
    context_frames,
    key_mask,
    value_weight,
    out_weight,
    expand_weight,
    depth_weight,
    norm_scale,
    norm_shift,
    project_weight,
):
    rows, width = span_frames.shape
    frames = key_rows.shape[0]
    half = width // CORES
    group = max(1, min(n, 64 // rows))
    stat_width = rows * 2 * (HEADS // CORES)
    vmem = pltpu.VMEM
    dma = pltpu.SemaphoreType.DMA
    args = (
        span_frames,
        query_rows,
        key_rows,
        context_frames,
        key_mask.reshape(1, frames),
        value_weight,
        out_weight,
        expand_weight,
        depth_weight,
        norm_scale.reshape(1, width),
        norm_shift.reshape(1, width),
        project_weight,
    )
    return pl.pallas_call(
        functools.partial(layer_kernel, n, group),
        out_shape=pltpu.VMEM((rows, width), BF16),
        in_specs=[pl.BlockSpec(memory_space=pl.ANY)] * len(args),
        out_specs=pl.BlockSpec(memory_space=pltpu.VMEM),
        scratch_shapes=[
            vmem((rows, width), BF16),
            vmem((CORES, rows, half), BF16),
            vmem((CORES, frames, half), BF16),
            vmem((frames, width), BF16),
            vmem((CORES, 1, frames), jnp.int32),
            vmem(value_weight.shape, BF16),
            vmem(out_weight.shape, BF16),
            vmem(expand_weight.shape, BF16),
            vmem(depth_weight.shape, F32),
            vmem((1, width), F32),
            vmem((1, width), F32),
            vmem(project_weight.shape, BF16),
            vmem((frames, half), BF16),
            vmem((CORES, frames, half), BF16),
            vmem((n, rows, half), BF16),
            vmem((n, rows, half), BF16),
            vmem((n, rows, half), BF16),
            vmem((n, 1, stat_width), F32),
            vmem((n, 1, stat_width), F32),
            vmem((stat_width, 2 * half), BF16),
            vmem((1, CORES * frames), F32),
            vmem((rows, width), BF16),
            vmem((2, rows, width), BF16),
            vmem((3 * rows, width), F32),
            dma((16,)),
            dma((n,)),
            dma((n,)),
            dma((n,)),
            dma((n,)),
            dma((n,)),
            dma((n,)),
            dma((3,)),
            dma((3,)),
            dma((2,)),
            dma((2,)),
        ],
        compiler_params=pltpu.CompilerParams(collective_id=0, has_side_effects=True),
    )(*args)


def solution(mesh):
    rows = P(("groups", "seq"), None)
    in_specs = (rows, rows, rows, rows, P(("groups", "seq"))) + (P(),) * 7
    return jax.shard_map(
        functools.partial(body, mesh.shape["seq"]),
        mesh=mesh,
        in_specs=in_specs,
        out_specs=rows,
        check_vma=False,
    )
```

```python
import functools

import jax
import jax.numpy as jnp
from jax import lax
from jax.experimental import pallas as pl
from jax.experimental.pallas import tpu as pltpu
from jax.sharding import PartitionSpec as P

HEADS = 8
CORES = 2
MESH = pl.DeviceIdType.MESH
F32 = jnp.float32
BF16 = jnp.bfloat16


def dot(a, b):
    return jnp.dot(a, b, preferred_element_type=F32)


def layer_kernel(
    n,
    group,
    span_hbm,
    query_hbm,
    key_hbm,
    context_hbm,
    mask_hbm,
    value_w_hbm,
    out_w_hbm,
    expand_w_hbm,
    depth_hbm,
    scale_hbm,
    shift_hbm,
    project_w_hbm,
    out_ref,
    span,
    own_query,
    keys,
    context,
    mask,
    value_w,
    out_w,
    expand_w,
    depth,
    norm_scale,
    norm_shift,
    project_w,
    value_out,
    values,
    queries,
    partial_out,
    partials,
    stat_out,
    stat_in,
    spread,
    bias,
    gated,
    halo,
    padded,
    load_sem,
    query_send,
    query_recv,
    part_send,
    part_recv,
    stat_send,
    stat_recv,
    pair_send,
    pair_recv,
    halo_send,
    halo_recv,
):
    me = lax.axis_index("seq")
    core = lax.rem(me, CORES)
    other = 1 - core
    pair = me - core + other
    rows, width = span.shape
    half = width // CORES
    frames = context.shape[0]
    heads = HEADS // CORES
    head_dim = width // HEADS
    block_rows = group * rows
    blocks = n // group
    unroll = n <= 32

    barrier = pltpu.get_barrier_semaphore()

    def greet(step, carry):
        peer = lax.rem(me + step, n)
        pl.semaphore_signal(barrier, inc=1, device_id={"seq": peer}, device_id_type=MESH)
        return carry

    lax.fori_loop(1, n, greet, 0, unroll=unroll)

    def columns(index):
        return pl.ds(pl.multiple_of(index * half, half), half)

    loads = []

    def load(src, dst):
        copy = pltpu.make_async_copy(src, dst, load_sem.at[len(loads)])
        copy.start()
        loads.append(copy)
        return copy

    load_context = load(context_hbm, context)
    load_value_w = load(value_w_hbm, value_w)
    load_query = [load(query_hbm.at[:, i * half : (i + 1) * half], own_query.at[i]) for i in range(CORES)]
    load_mask = load(mask_hbm, mask.at[core])
    load_keys = load(key_hbm.at[:, columns(core)], keys.at[core])
    load_rest = [
        load(src, dst)
        for src, dst in (
            (span_hbm, span),
            (out_w_hbm, out_w),
            (expand_w_hbm, expand_w),
            (depth_hbm, depth),
            (scale_hbm, norm_scale),
            (shift_hbm, norm_shift),
            (project_w_hbm, project_w),
        )
    ]

    load_context.wait()
    load_value_w.wait()
    value_out[...] = dot(context[...], value_w[:, columns(other)]).astype(BF16)
    for copy in load_query:
        copy.wait()
    load_mask.wait()

    values[core] = dot(context[...], value_w[:, columns(core)]).astype(BF16)
    fields = 2 * heads
    stat_width = stat_out.shape[-1]
    slot = lax.rem(lax.broadcasted_iota(jnp.int32, (stat_width, 2 * half), 0), fields)
    target = lax.broadcasted_iota(jnp.int32, (stat_width, 2 * half), 1)
    wanted = lax.rem(target, half) // head_dim * 2 + target // half
    spread[...] = jnp.where(slot == wanted, 1.0, 0.0).astype(BF16)
    field = lax.rem(lax.broadcasted_iota(jnp.int32, (1, stat_width), 1), fields)
    own_row = (
        lax.broadcasted_iota(jnp.int32, (1, rows, stat_width), 2) // fields
        == lax.broadcasted_iota(jnp.int32, (1, rows, stat_width), 1)
    )

    pl.semaphore_wait(barrier, n - 1)

    def remote(src, dst, send, recv, peer):
        return pltpu.make_async_remote_copy(
            src_ref=src,
            dst_ref=dst,
            send_sem=send,
            recv_sem=recv,
            device_id={"seq": peer},
            device_id_type=MESH,
        )

    def query_copy(peer, slot, sem_index):
        return remote(
            own_query.at[lax.rem(peer, CORES)],
            queries.at[slot],
            query_send.at[sem_index],
            query_recv.at[slot],
            peer,
        )

    def part_copies(peer, place):
        return (
            remote(
                stat_out.at[peer], stat_in.at[place], stat_send.at[peer], stat_recv.at[place], peer
            ),
            remote(
                partial_out.at[peer], partials.at[place], part_send.at[peer], part_recv.at[place], peer
            ),
        )

    key_copy = remote(
        key_hbm.at[:, columns(other)], keys.at[core], pair_send.at[0], pair_recv.at[0], pair
    )
    mask_copy = remote(mask.at[core], mask.at[core], pair_send.at[1], pair_recv.at[1], pair)
    value_copy = remote(value_out, values.at[core], pair_send.at[2], pair_recv.at[2], pair)
    key_copy.start()
    mask_copy.start()

    first_block = me // group
    heading = 1 - 2 * (2 * first_block // blocks)

    def send_query(step, carry):
        spot = step
        peer = lax.rem(first_block + heading * (spot // group) + blocks, blocks) * group + lax.rem(me + lax.rem(spot, group), group)

        @pl.when(peer != me)
        def _():
            query_copy(peer, me, peer).start()

        return carry

    lax.fori_loop(0, n, send_query, 0, unroll=unroll)
    value_copy.start()

    queries[me] = own_query[core]
    load_keys.wait()
    remote(keys.at[other], keys.at[other], pair_send.at[0], pair_recv.at[0], pair).wait_recv()
    remote(mask.at[other], mask.at[other], pair_send.at[1], pair_recv.at[1], pair).wait_recv()
    for i in range(CORES):
        bias[:, i * frames : (i + 1) * frames] = jnp.where(mask[i] > 0, 0.0, -1e30)

    head_lane = lax.broadcasted_iota(jnp.int32, (1, half), 1) // head_dim

    def attend(step, carry):
        block = lax.rem(first_block + heading * step + blocks, blocks)
        for i in range(group):
            source = block * group + i

            @pl.when(source != me)
            def _():
                query_copy(pair, source, source).wait_recv()

        query = queries[pl.ds(block * group, group)].reshape(block_rows, half)
        stacked = jnp.concatenate(
            [query * jnp.where(head_lane == h, head_dim**-0.5, 0.0).astype(BF16) for h in range(heads)],
            axis=0,
        )
        scores = (
            lax.dot_general(
                stacked,
                keys[...].reshape(CORES * frames, half),
                (((1,), (1,)), ((), ())),
                preferred_element_type=F32,
            )
            + bias[...]
        )
        shift = jnp.ceil(jnp.max(scores, axis=1, keepdims=True) * 0.25)
        shift = (shift.astype(BF16).astype(F32)) * 4.0
        weights = jnp.exp(scores - shift)
        total = jnp.sum(weights, axis=1, keepdims=True)

        @pl.when(step == 0)
        def _():
            remote(
                values.at[other], values.at[other], pair_send.at[2], pair_recv.at[2], pair
            ).wait_recv()

        numer = dot(weights.astype(BF16), values[...].reshape(CORES * frames, half))
        packed = jnp.zeros((block_rows, half), F32)
        stats = jnp.zeros((block_rows, stat_width), F32)
        for h in range(heads):
            part = slice(h * block_rows, (h + 1) * block_rows)
            packed = jnp.where(head_lane == h, numer[part], packed)
            stats = jnp.where(field == 2 * h, shift[part], stats)
            stats = jnp.where(field == 2 * h + 1, total[part], stats)
        stats = jnp.where(own_row, stats.reshape(group, rows, stat_width), 0.0)
        stat_out[pl.ds(block * group, group)] = jnp.sum(stats, axis=1, keepdims=True)
        partial_out[pl.ds(block * group, group)] = packed.astype(BF16).reshape(group, rows, half)
        for i in range(group):
            peer = block * group + i

            @pl.when(peer != me)
            def _():
                for copy in part_copies(peer, me):
                    copy.start()

        return carry

    lax.fori_loop(0, blocks, attend, 0, unroll=unroll)
    partials[me] = partial_out[me]
    stat_in[me] = stat_out[me]

    for copy in load_rest:
        copy.wait()

    def take_part(step, carry):
        peer = lax.rem(me + step, n)
        for copy in part_copies(peer, peer):
            copy.wait_recv()
        return carry

    lax.fori_loop(1, n, take_part, 0, unroll=unroll)

    chips = n // CORES
    stats = jnp.where(own_row, stat_in[...], 0.0).reshape(n * rows, stat_width)
    high = stats.astype(BF16)
    low = (stats - high.astype(F32)).astype(BF16)
    stats = dot(high, spread[...]) + dot(low, spread[...])
    stats = stats.reshape(chips, CORES, rows, 2 * half)
    numers = partials[...].astype(F32).reshape(chips, CORES, rows, half)
    shifts = stats[:, :, :, :half]
    shares = jnp.exp(shifts - jnp.max(shifts, axis=0, keepdims=True))
    attended = jnp.sum(shares * numers, axis=0) / jnp.sum(shares * stats[:, :, :, half:], axis=0)
    attended = jnp.concatenate([attended[i] for i in range(CORES)], axis=1).astype(BF16)

    wide = span[...].astype(F32) + dot(attended, out_w[...])
    mixed = wide.astype(BF16).astype(F32)
    centre = jnp.mean(mixed, axis=1, keepdims=True)
    deviation = mixed - centre
    variance = jnp.mean(deviation * deviation, axis=1, keepdims=True)
    normed = (deviation / jnp.sqrt(variance + 1e-05)).astype(BF16)
    expanded = dot(normed, expand_w[...])
    gated[...] = (expanded[:, :width] * jax.nn.sigmoid(expanded[:, width:])).astype(BF16)

    def halo_copy(side, peer):
        return remote(gated, halo.at[side], halo_send.at[side], halo_recv.at[side], peer)

    @pl.when(me < n - 1)
    def _():
        halo_copy(0, me + 1).start()

    @pl.when(me > 0)
    def _():
        halo_copy(1, me - 1).start()

    padded[rows : 2 * rows] = gated[...].astype(F32)

    @pl.when(me > 0)
    def _():
        halo_copy(0, me - 1).wait_recv()
        padded[:rows] = halo[0].astype(F32)

    @pl.when(me == 0)
    def _():
        padded[:rows] = jnp.zeros((rows, width), F32)

    @pl.when(me < n - 1)
    def _():
        halo_copy(1, me + 1).wait_recv()
        padded[2 * rows :] = halo[1].astype(F32)

    @pl.when(me == n - 1)
    def _():
        padded[2 * rows :] = jnp.zeros((rows, width), F32)

    taps = depth.shape[0]
    first = rows - taps // 2
    conv = jnp.zeros((rows, width), F32)
    for tap in range(taps):
        conv = conv + padded[first + tap : first + tap + rows] * depth[tap : tap + 1]
    normal = conv * norm_scale[...] + norm_shift[...]
    activated = (normal * jax.nn.sigmoid(normal)).astype(BF16)
    out_ref[...] = (mixed + dot(activated, project_w[...])).astype(BF16)

    def finish(step, carry):
        peer = lax.rem(me + step, n)
        query_copy(peer, me, peer).wait_send()
        for copy in part_copies(peer, me):
            copy.wait_send()
        return carry

    lax.fori_loop(1, n, finish, 0, unroll=unroll)
    key_copy.wait_send()
    mask_copy.wait_send()
    value_copy.wait_send()

    @pl.when(me < n - 1)
    def _():
        halo_copy(0, me + 1).wait_send()

    @pl.when(me > 0)
    def _():
        halo_copy(1, me - 1).wait_send()


def body(
    n,
    span_frames,
    query_rows,
    key_rows,
    context_frames,
    key_mask,
    value_weight,
    out_weight,
    expand_weight,
    depth_weight,
    norm_scale,
    norm_shift,
    project_weight,
):
    rows, width = span_frames.shape
    frames = key_rows.shape[0]
    half = width // CORES
    group = max(1, min(n, 64 // rows))
    stat_width = rows * 2 * (HEADS // CORES)
    vmem = pltpu.VMEM
    dma = pltpu.SemaphoreType.DMA
    args = (
        span_frames,
        query_rows,
        key_rows,
        context_frames,
        key_mask.reshape(1, frames),
        value_weight,
        out_weight,
        expand_weight,
        depth_weight,
        norm_scale.reshape(1, width),
        norm_shift.reshape(1, width),
        project_weight,
    )
    return pl.pallas_call(
        functools.partial(layer_kernel, n, group),
        out_shape=pltpu.VMEM((rows, width), BF16),
        in_specs=[pl.BlockSpec(memory_space=pl.ANY)] * len(args),
        out_specs=pl.BlockSpec(memory_space=pltpu.VMEM),
        scratch_shapes=[
            vmem((rows, width), BF16),
            vmem((CORES, rows, half), BF16),
            vmem((CORES, frames, half), BF16),
            vmem((frames, width), BF16),
            vmem((CORES, 1, frames), jnp.int32),
            vmem(value_weight.shape, BF16),
            vmem(out_weight.shape, BF16),
            vmem(expand_weight.shape, BF16),
            vmem(depth_weight.shape, F32),
            vmem((1, width), F32),
            vmem((1, width), F32),
            vmem(project_weight.shape, BF16),
            vmem((frames, half), BF16),
            vmem((CORES, frames, half), BF16),
            vmem((n, rows, half), BF16),
            vmem((n, rows, half), BF16),
            vmem((n, rows, half), BF16),
            vmem((n, 1, stat_width), F32),
            vmem((n, 1, stat_width), F32),
            vmem((stat_width, 2 * half), BF16),
            vmem((1, CORES * frames), F32),
            vmem((rows, width), BF16),
            vmem((2, rows, width), BF16),
            vmem((3 * rows, width), F32),
            dma((16,)),
            dma((n,)),
            dma((n,)),
            dma((n,)),
            dma((n,)),
            dma((n,)),
            dma((n,)),
            dma((3,)),
            dma((3,)),
            dma((2,)),
            dma((2,)),
        ],
        compiler_params=pltpu.CompilerParams(collective_id=0, has_side_effects=True),
    )(*args)


def solution(mesh):
    rows = P(("groups", "seq"), None)
    in_specs = (rows, rows, rows, rows, P(("groups", "seq"))) + (P(),) * 7
    return jax.shard_map(
        functools.partial(body, mesh.shape["seq"]),
        mesh=mesh,
        in_specs=in_specs,
        out_specs=rows,
        check_vma=False,
    )
```
